512 devices in a mesh: pipe: 4 (over z_hi), ctx: 32 (over x, y, core), chan: 4 (over z_lo).
Axes of the slice: x: 4, y: 4, z: 16 (z_hi: 4, z_lo: 4; z = z_hi * 4 + z_lo), core: 2. Of those that a mesh axis runs over, the one named last changes fastest.
Arguments:
- handed_back: bfloat16 [4, 1, 4096, 4096], P('pipe', None, 'chan', 'ctx'), may hold values from -6 to 6
- gate_q: bfloat16 [4, 1, 4096, 4096], P('pipe', None, 'chan', 'ctx'), may hold values from -6 to 6
- key_k: bfloat16 [4, 1, 4096, 4096], P('pipe', None, 'chan', 'ctx'), may hold values from -6 to 6
- input_x: bfloat16 [4, 1, 4096, 4096], P('pipe', None, 'chan', 'ctx'), may hold values from -6 to 6
- filter_h: bfloat16 [4, 4096, 4096], P('pipe', 'chan', 'ctx'), may hold values from -1.5 to 1.5
- doc_lengths: int32 [1, 8], replicated, may hold values from 1 to 1024, 4096 in all within a row
- section_layers: int32 [4], replicated, may hold values from 2 to 12
Outputs:
- grad_input: bfloat16 [4, 1, 4096, 4096], P('pipe', None, 'chan', 'ctx')
- grad_gate: bfloat16 [4, 1, 4096, 4096], P('pipe', None, 'chan', 'ctx')
- grad_key: bfloat16 [4, 1, 4096, 4096], P('pipe', None, 'chan', 'ctx')
- grad_filter: float32 [4, 4096, 4096], P('pipe', 'chan', 'ctx')
The draws below stay inside these ranges and needn't reach their ends.
Inputs may be any that keep to these rules, and one draw needn't show every extreme that they name: `doc_lengths`: positions from 4096 minus a row's last entry onward are padding.
All inputs are finite; a program needn't handle non-finite values.
Results may differ from the reference program's by a relative error of at most 0.0085.
Values may be sent and summed in bfloat16 or wider, within the bound.
A program may use at most 64 MiB of HBM per device.

```python
import math
import jax
import jax.numpy as jnp
import numpy as np
from jax import lax

C = 4096
B = 1
NDOC = 8
SEQ = 4096
PIPE = 4


def draw_filter_h(key, part):
    rate_key, rough_key = jax.random.split(jax.random.fold_in(key, 7), 2)
    lowest = math.log(0.3 / SEQ)
    highest = math.log(1.0 / 30.0)
    rough_part = jnp.clip(jax.random.normal(rough_key, (PIPE, C, SEQ), jnp.float32), -4.0, 4.0)
    decay_rates = jnp.exp(jax.random.uniform(rate_key, (PIPE, C, 1), jnp.float32, lowest, highest))
    positions = jnp.arange(SEQ, dtype=jnp.float32)[None, None, :]
    amplitude = jnp.sqrt(2.0 * decay_rates / (1.0 - jnp.exp(-2.0 * decay_rates * SEQ)))
    values = amplitude * rough_part * jnp.exp(-decay_rates * positions)
    return values.astype(jnp.bfloat16)


def draw_section_layers(key, part):
    base_key, shuffle_key = jax.random.split(jax.random.fold_in(key, 13))
    counts = jax.random.randint(base_key, (PIPE,), 2, 13, dtype=jnp.int32)
    shuffled = jax.random.permutation(shuffle_key, PIPE)
    counts = counts.at[shuffled[0]].set(2)
    counts = counts.at[shuffled[1]].set(12)
    return counts


def shard_levels(own_key, shape, shards, low, high):
    gain = 1.0
    for dim, blocks in shards:
        heights = jax.random.uniform(jax.random.fold_in(jax.random.fold_in(own_key, 6), dim), (blocks,), jnp.float32, low / len(shards), high / len(shards))
        gain = gain * jnp.repeat(jnp.exp(heights), shape[dim] // blocks).reshape((-1,) + (1,) * (len(shape) - 1 - dim))
    return gain


def split_up(amount, total, bound, skew):
    weights = [(1 << 20) // math.isqrt(grade ** skew) + 1 for grade in range(2, amount + 1)]
    spare, given = total - bound - (amount - 1), [1] * (amount - 1)
    while spare > 0:
        movable = [i for i in range(amount - 1) if given[i] < bound]
        mass, left = sum([weights[i] for i in movable]), spare
        for i in movable:
            addition = min(bound - given[i], max(1, left * weights[i] // mass), spare)
            given[i] = given[i] + addition
            spare = spare - addition
    return np.array([bound] + given)


def uneven_parts(stream_key, count, total, most, skew):
    if count == 2:
        one = jax.random.randint(stream_key, (), max(1, total - most), min(most, total - 1) + 1)
        return jnp.stack([one, total - one])
    sizes = jnp.asarray(split_up(count, total, most, skew), jnp.int32)
    couples = (count - 1) // 2
    donor, receiver = sizes[1:1 + 2 * couples:2], sizes[2:2 + 2 * couples:2]
    slack = jnp.minimum(donor - 1, most - receiver)
    moved = jax.random.randint(jax.random.fold_in(stream_key, 1), (couples,), 0, 1 << 20) % (slack + 1)
    sizes = sizes.at[1:1 + 2 * couples:2].set(donor - moved).at[2:2 + 2 * couples:2].set(receiver + moved)
    return sizes[jax.random.permutation(jax.random.fold_in(stream_key, 2), count)]


def noise(own_key, dims, deviation, most, cuts=(), kind=jnp.bfloat16):
    drawn = jax.random.normal(own_key, dims, jnp.float32) * deviation
    if len(cuts) > 0:
        drawn = shard_levels(own_key, dims, cuts, -0.22, 0.18) * drawn
    return jnp.clip(drawn, min=-most, max=most).astype(kind)


def setup_inputs(seed: int = 0) -> dict:
    key_list = jax.random.split(jax.random.key(seed), 8)
    return {
        "handed_back": noise(key_list[0], (PIPE, B, C, SEQ), 1.0, 6.0, ((0, 4), (2, 4), (3, 32))),
        "gate_q": noise(key_list[1], (PIPE, B, C, SEQ), 1.0, 6.0, ((0, 4), (2, 4), (3, 32))),
        "key_k": noise(key_list[2], (PIPE, B, C, SEQ), 1.0, 6.0, ((0, 4), (2, 4), (3, 32))),
        "input_x": noise(key_list[3], (PIPE, B, C, SEQ), 1.0, 6.0, ((0, 4), (2, 4), (3, 32))),
        "filter_h": draw_filter_h(jax.random.fold_in(key_list[7], 71), 0),
        "doc_lengths": jax.vmap(lambda own: uneven_parts(own, NDOC, SEQ, SEQ // 4, 2))(jax.random.split(key_list[5], B)).reshape((B, NDOC)).astype(jnp.int32),
        "section_layers": draw_section_layers(jax.random.fold_in(key_list[7], 71), 0),
    }


def block_backward(pieces, live_mask, branch_scale):
    incoming, gate_vals, key_vals, input_vals, filt = pieces
    grad32 = incoming.astype(jnp.float32)
    gate32 = gate_vals.astype(jnp.float32)
    key32 = key_vals.astype(jnp.float32)
    input32 = input_vals.astype(jnp.float32)
    length = incoming.shape[-1]
    span_len = 2 * length
    product = (key32 * input32 * live_mask).astype(jnp.bfloat16)
    branch_grad = (branch_scale * gate32 * grad32).astype(jnp.bfloat16)
    filt_spec = jnp.fft.rfft(filt.astype(jnp.float32), n=span_len, axis=-1)
    prod_spec = jnp.fft.rfft(product.astype(jnp.float32), n=span_len, axis=-1)
    grad_spec = jnp.fft.rfft(branch_grad.astype(jnp.float32), n=span_len, axis=-1)
    conv = jnp.fft.irfft(filt_spec[None] * prod_spec, n=span_len, axis=-1)[..., :length].astype(jnp.bfloat16)
    corr = jnp.fft.irfft(jnp.conj(filt_spec)[None] * grad_spec, n=span_len, axis=-1)[..., :length].astype(jnp.bfloat16)
    summed = lax.optimization_barrier(jnp.sum(jnp.conj(prod_spec) * grad_spec, axis=0))
    filter_grad = jnp.fft.irfft(summed, n=span_len, axis=-1)[..., :length]
    filter_grad = filter_grad / jnp.sqrt(jnp.float32(incoming.shape[0] * length))
    conv32 = conv.astype(jnp.float32)
    corr32 = corr.astype(jnp.float32)
    grad_gate = (branch_scale * grad32 * conv32).astype(jnp.bfloat16)
    grad_key = (corr32 * input32 * live_mask).astype(jnp.bfloat16)
    grad_input = (grad32 + corr32 * key32 * live_mask).astype(jnp.bfloat16)
    return (grad_input, grad_gate, grad_key, filter_grad.astype(jnp.float32))

def to_blocks(array, group_size):
    count = array.shape[0]
    shaped = array.reshape(count, array.shape[1] // group_size, group_size, array.shape[2])
    return jnp.transpose(shaped, (1, 0, 2, 3))

def from_blocks(array):
    merged = jnp.transpose(array, (1, 0, 2, 3))
    return merged.reshape(merged.shape[0], merged.shape[1] * merged.shape[2], merged.shape[3])

def reference(handed_back, gate_q, key_k, input_x, filter_h, doc_lengths, section_layers):
    group_size = 128 if C % 128 == 0 else C
    positions = jnp.arange(SEQ, dtype=jnp.int32)
    live_limit = SEQ - doc_lengths[:, NDOC - 1]
    live_mask = (positions[None, :] < live_limit[:, None]).astype(jnp.float32)[:, None, :]
    inputs_out, gates_out, keys_out, filters_out = ([], [], [], [])
    for section in range(PIPE):
        branch_scale = 1.0 / jnp.sqrt(section_layers[section].astype(jnp.float32))
        incoming = handed_back[(section + 1) % PIPE]
        pieces = (to_blocks(incoming, group_size), to_blocks(gate_q[section], group_size), to_blocks(key_k[section], group_size), to_blocks(input_x[section], group_size), filter_h[section].reshape(C // group_size, group_size, SEQ))
        results = lax.map(lambda piece: block_backward(piece, live_mask, branch_scale), pieces)
        inputs_out.append(from_blocks(results[0]))
        gates_out.append(from_blocks(results[1]))
        keys_out.append(from_blocks(results[2]))
        filters_out.append(results[3].reshape(C, SEQ))
    return (jnp.stack(inputs_out), jnp.stack(gates_out), jnp.stack(keys_out), jnp.stack(filters_out))
```

```python
import functools
import math

import jax
import jax.numpy as jnp
import numpy as np
from jax import lax
from jax.experimental import pallas as pl
from jax.experimental.pallas import tpu as pltpu
from jax.sharding import PartitionSpec as P

GROUP = 8


def halves(table):
    top = table.astype(jnp.bfloat16)
    rest = (table - top.astype(np.float64)).astype(jnp.bfloat16)
    return np.stack([top, rest])


@functools.lru_cache(maxsize=None)
def tables(blocks, width):
    length = blocks * width
    turn = 2.0 * math.pi
    row = np.arange(blocks)[:, None]
    quarter = np.arange(blocks)[:, None] + 0.25
    outer = turn * quarter * row.T / blocks
    wave = np.concatenate([np.cos(outer), -np.sin(outer)])
    spread = np.kron(wave, np.eye(GROUP))
    twist = np.repeat(turn * quarter * np.arange(width)[None, :] / length, GROUP, axis=0)
    lane = np.arange(width)
    inner = turn * ((lane[:, None] * lane[None, :]) % width) / width
    cos, sin = np.cos(inner), np.sin(inner)
    ahead = np.block([[cos, -sin], [sin, cos]])
    back = np.block([[cos, sin], [-sin, cos]])
    turns = np.stack([np.cos(twist), -np.sin(twist)]).astype(np.float32)
    return (halves(spread), halves(spread.T / length), halves(ahead), halves(back), turns)


def fixed_left(table_ref, right):
    return jnp.dot(table_ref[0], right, preferred_element_type=jnp.float32) + jnp.dot(
        table_ref[1], right, preferred_element_type=jnp.float32
    )


def fixed_right(left, table_ref):
    return jnp.dot(left, table_ref[0], preferred_element_type=jnp.float32) + jnp.dot(
        left, table_ref[1], preferred_element_type=jnp.float32
    )


def transform(wide_ref, spec_ref, spread_ref, ahead_ref, turns_ref):
    blocks, channels, width = wide_ref.shape
    rows = blocks * GROUP
    for pair in range(channels // (2 * GROUP)):
        chunk = wide_ref[:, 2 * GROUP * pair : 2 * GROUP * (pair + 1), :].astype(jnp.float32)
        sides = [chunk[:, :GROUP, :].reshape(rows, width), chunk[:, GROUP:, :].reshape(rows, width)]
        mixed = fixed_left(spread_ref, jnp.concatenate(sides, axis=1).astype(jnp.bfloat16))
        for side in range(2):
            part = mixed[:, side * width : (side + 1) * width]
            part_re, part_im = part[:rows], part[rows:]
            turned = jnp.concatenate(
                [
                    part_re * turns_ref[0] - part_im * turns_ref[1],
                    part_re * turns_ref[1] + part_im * turns_ref[0],
                ],
                axis=1,
            )
            spec_ref[2 * pair + side] = fixed_right(turned.astype(jnp.bfloat16), ahead_ref)


def multiply(left_ref, right_ref, conjugate, wide_ref, gather_ref, back_ref, turns_ref):
    blocks, channels, width = wide_ref.shape
    rows = blocks * GROUP
    for pair in range(channels // (2 * GROUP)):
        sides = []
        for side in range(2):
            left, right = left_ref[2 * pair + side], right_ref[2 * pair + side]
            left_re, left_im = left[:, :width], left[:, width:]
            right_re, right_im = right[:, :width], right[:, width:]
            if conjugate:
                left_im = -left_im
            both = jnp.concatenate(
                [left_re * right_re - left_im * right_im, left_re * right_im + left_im * right_re],
                axis=1,
            )
            part = fixed_right(both.astype(jnp.bfloat16), back_ref)
            part_re, part_im = part[:, :width], part[:, width:]
            sides.append(
                jnp.concatenate(
                    [
                        part_re * turns_ref[0] + part_im * turns_ref[1],
                        part_im * turns_ref[0] - part_re * turns_ref[1],
                    ],
                    axis=0,
                )
            )
        signal = fixed_left(gather_ref, jnp.concatenate(sides, axis=1).astype(jnp.bfloat16))
        outs = [signal[:, s * width : (s + 1) * width].reshape(blocks, GROUP, width) for s in range(2)]
        chunk = jnp.concatenate(outs, axis=1).astype(jnp.bfloat16)
        wide_ref[:, 2 * GROUP * pair : 2 * GROUP * (pair + 1), :] = chunk


def kernel(
    filter_ref, prod_ref, grad_ref, spread_ref, gather_ref, ahead_ref, back_ref, turns_ref,
    conv_ref, corr_ref, lag_ref, filter_spec, prod_spec, grad_spec,
):
    transform(filter_ref, filter_spec, spread_ref, ahead_ref, turns_ref)
    transform(prod_ref, prod_spec, spread_ref, ahead_ref, turns_ref)
    transform(grad_ref, grad_spec, spread_ref, ahead_ref, turns_ref)
    multiply(filter_spec, prod_spec, False, conv_ref, gather_ref, back_ref, turns_ref)
    multiply(filter_spec, grad_spec, True, corr_ref, gather_ref, back_ref, turns_ref)
    multiply(prod_spec, grad_spec, True, lag_ref, gather_ref, back_ref, turns_ref)


def spectra(filter_wide, prod_wide, grad_wide):
    blocks, channels, width = filter_wide.shape
    out = jax.ShapeDtypeStruct((blocks, channels, width), jnp.bfloat16)
    spec = pltpu.VMEM((channels // GROUP, blocks * GROUP, 2 * width), jnp.float32)
    held = pl.BlockSpec(memory_space=pltpu.VMEM)
    return pl.pallas_call(
        kernel,
        out_shape=(out, out, out),
        in_specs=[held] * 8,
        out_specs=(held, held, held),
        scratch_shapes=[spec, spec, spec],
        compiler_params=pltpu.CompilerParams(vmem_limit_bytes=48 * 1024 * 1024),
    )(filter_wide, prod_wide, grad_wide, *tables(blocks, width))


def exchange(value):
    return lax.all_to_all(value, "ctx", split_axis=0, concat_axis=0, tiled=True)


def body(handed_back, gate_q, key_k, input_x, filter_h, doc_lengths, section_layers):
    channels, width = gate_q.shape[2:]
    blocks = lax.axis_size("ctx")
    pipe = lax.axis_size("pipe")
    length = blocks * width
    shape = (blocks, channels // blocks, width)
    layers = section_layers[lax.axis_index("pipe")]
    scale = 1.0 / jnp.sqrt(layers.astype(jnp.float32))
    spots = lax.axis_index("ctx") * width + jnp.arange(width, dtype=jnp.int32)
    live = (spots < length - doc_lengths[0, -1]).astype(jnp.float32)
    incoming = lax.ppermute(handed_back, "pipe", [(s, (s - 1) % pipe) for s in range(pipe)])
    key32 = key_k.reshape(shape).astype(jnp.float32)
    input32 = input_x.reshape(shape).astype(jnp.float32)
    product = (key32 * input32 * live).astype(jnp.bfloat16)
    first = exchange(jnp.stack([product, filter_h.reshape(shape)], axis=1))
    grad32 = incoming.reshape(shape).astype(jnp.float32)
    gate32 = gate_q.reshape(shape).astype(jnp.float32)
    branch = exchange((scale * gate32 * grad32).astype(jnp.bfloat16))
    results = spectra(first[:, 1], first[:, 0], branch)
    home = exchange(jnp.stack(results, axis=1)).astype(jnp.float32)
    conv32, corr32, lags = home[:, 0], home[:, 1], home[:, 2]
    grad_gate = (scale * grad32 * conv32).astype(jnp.bfloat16)
    grad_key = (corr32 * input32 * live).astype(jnp.bfloat16)
    grad_input = (grad32 + corr32 * key32 * live).astype(jnp.bfloat16)
    grad_filter = lags / math.sqrt(length)
    flat = gate_q.shape
    return (
        grad_input.reshape(flat),
        grad_gate.reshape(flat),
        grad_key.reshape(flat),
        grad_filter.reshape(filter_h.shape),
    )


def solution(mesh):
    return jax.shard_map(
        body,
        mesh=mesh,
        in_specs=(
            P("pipe", None, "chan", "ctx"),
            P("pipe", None, "chan", "ctx"),
            P("pipe", None, "chan", "ctx"),
            P("pipe", None, "chan", "ctx"),
            P("pipe", "chan", "ctx"),
            P(),
            P(),
        ),
        out_specs=(
            P("pipe", None, "chan", "ctx"),
            P("pipe", None, "chan", "ctx"),
            P("pipe", None, "chan", "ctx"),
            P("pipe", "chan", "ctx"),
        ),
        check_vma=False,
    )
```

```python
import functools
import math

import jax
import jax.numpy as jnp
import numpy as np
from jax import lax
from jax.experimental import pallas as pl
from jax.experimental.pallas import tpu as pltpu
from jax.sharding import PartitionSpec as P

GROUP = 8


def halves(table):
    top = table.astype(jnp.bfloat16)
    rest = (table - top.astype(np.float64)).astype(jnp.bfloat16)
    return np.stack([top, rest])


@functools.lru_cache(maxsize=None)
def tables(blocks, width):
    length = blocks * width
    turn = 2.0 * math.pi
    row = np.arange(blocks)[:, None]
    quarter = np.arange(blocks)[:, None] + 0.25
    outer = turn * quarter * row.T / blocks
    wave = np.concatenate([np.cos(outer), -np.sin(outer)])
    spread = np.kron(wave, np.eye(GROUP))
    twist = np.repeat(turn * quarter * np.arange(width)[None, :] / length, GROUP, axis=0)
    lane = np.arange(width)
    inner = turn * ((lane[:, None] * lane[None, :]) % width) / width
    cos, sin = np.cos(inner), np.sin(inner)
    ahead = np.block([[cos, -sin], [sin, cos]])
    back = np.block([[cos, sin], [-sin, cos]])
    turns = np.stack([np.cos(twist), -np.sin(twist)]).astype(np.float32)
    return (halves(spread), halves(spread.T / length), halves(ahead), halves(back), turns)


def fixed_left(table_ref, right):
    return jnp.dot(table_ref[0], right, preferred_element_type=jnp.float32) + jnp.dot(
        table_ref[1], right, preferred_element_type=jnp.float32
    )


def fixed_right(left, table_ref):
    return jnp.dot(left, table_ref[0], preferred_element_type=jnp.float32) + jnp.dot(
        left, table_ref[1], preferred_element_type=jnp.float32
    )


def transform(wide_ref, spec_ref, pairs, spread_ref, ahead_ref, turns_ref):
    blocks, channels, width = wide_ref.shape
    rows = blocks * GROUP
    for pair in pairs:
        chunk = wide_ref[:, 2 * GROUP * pair : 2 * GROUP * (pair + 1), :].astype(jnp.float32)
        sides = [chunk[:, :GROUP, :].reshape(rows, width), chunk[:, GROUP:, :].reshape(rows, width)]
        mixed = fixed_left(spread_ref, jnp.concatenate(sides, axis=1).astype(jnp.bfloat16))
        for side in range(2):
            part = mixed[:, side * width : (side + 1) * width]
            part_re, part_im = part[:rows], part[rows:]
            turned = jnp.concatenate(
                [
                    part_re * turns_ref[0] - part_im * turns_ref[1],
                    part_re * turns_ref[1] + part_im * turns_ref[0],
                ],
                axis=1,
            )
            spec_ref[2 * pair + side] = fixed_right(turned.astype(jnp.bfloat16), ahead_ref)


def multiply(left_ref, right_ref, conjugate, wide_ref, pairs, gather_ref, back_ref, turns_ref):
    blocks, channels, width = wide_ref.shape
    rows = blocks * GROUP
    for pair in pairs:
        sides = []
        for side in range(2):
            left, right = left_ref[2 * pair + side], right_ref[2 * pair + side]
            left_re, left_im = left[:, :width], left[:, width:]
            right_re, right_im = right[:, :width], right[:, width:]
            if conjugate:
                left_im = -left_im
            both = jnp.concatenate(
                [left_re * right_re - left_im * right_im, left_re * right_im + left_im * right_re],
                axis=1,
            )
            part = fixed_right(both.astype(jnp.bfloat16), back_ref)
            part_re, part_im = part[:, :width], part[:, width:]
            sides.append(
                jnp.concatenate(
                    [
                        part_re * turns_ref[0] + part_im * turns_ref[1],
                        part_im * turns_ref[0] - part_re * turns_ref[1],
                    ],
                    axis=0,
                )
            )
        signal = fixed_left(gather_ref, jnp.concatenate(sides, axis=1).astype(jnp.bfloat16))
        outs = [signal[:, s * width : (s + 1) * width].reshape(blocks, GROUP, width) for s in range(2)]
        chunk = jnp.concatenate(outs, axis=1).astype(jnp.bfloat16)
        wide_ref[:, 2 * GROUP * pair : 2 * GROUP * (pair + 1), :] = chunk

MESH = pl.DeviceIdType.MESH
FILTER, PRODUCT, CONV, GRAD, CORR, LAG = 0, 1, 2, 3, 5, 7
STREAMS = 9


def kernel(
    docs_ref, layers_ref, handed_ref, gate_ref, key_ref, input_ref, filter_ref,
    spread_ref, gather_ref, ahead_ref, back_ref, turns_ref,
    incoming_ref, conv_ref, corr_ref, lag_ref, live_ref, scale_ref,
    prod_out, grad_out, filter_wide, prod_wide, grad_wide, conv_wide, corr_wide, lag_wide,
    filter_spec, prod_spec, grad_spec,
    send_sems, recv_sems, relay_send, relay_recv,
):
    blocks, channels, width = key_ref.shape
    me = lax.axis_index("ctx")
    section, sections = lax.axis_index("pipe"), lax.axis_size("pipe")
    before = lax.rem(section + sections - 1, sections)
    after = lax.rem(section + 1, sections)
    pairs = channels // (2 * GROUP)
    whole = pl.ds(0, channels)

    def part(pair):
        return pl.ds(2 * GROUP * pair, 2 * GROUP)

    def relay(pair):
        return pltpu.make_async_remote_copy(
            src_ref=handed_ref.at[:, part(pair), :],
            dst_ref=incoming_ref.at[:, part(pair), :],
            send_sem=relay_send.at[pair],
            recv_sem=relay_recv.at[pair],
            device_id={"pipe": before},
            device_id_type=MESH,
        )

    def scatter(source, target, span, stream):
        def step(index, carry):
            peer = lax.rem(me + index, blocks)
            pltpu.make_async_remote_copy(
                src_ref=source.at[peer, span, :],
                dst_ref=target.at[me, span, :],
                send_sem=send_sems.at[stream],
                recv_sem=recv_sems.at[stream],
                device_id={"ctx": peer},
                device_id_type=MESH,
            ).start()
            return carry

        lax.fori_loop(1, blocks, step, 0)
        target[me, span, :] = source[me, span, :]

    def settle(buffer, span, stream):
        others = buffer.at[pl.ds(0, blocks - 1), span, :]
        return pltpu.make_async_remote_copy(
            src_ref=others,
            dst_ref=others,
            send_sem=send_sems.at[stream],
            recv_sem=recv_sems.at[stream],
            device_id={"ctx": lax.rem(me + 1, blocks)},
            device_id_type=MESH,
        )

    barrier = pltpu.get_barrier_semaphore()

    def greet(index, carry):
        pl.semaphore_signal(
            barrier, inc=1, device_id={"ctx": lax.rem(me + index, blocks)}, device_id_type=MESH
        )
        return carry

    for neighbour in (before, after):
        pl.semaphore_signal(barrier, inc=1, device_id={"pipe": neighbour}, device_id_type=MESH)
    lax.fori_loop(1, blocks, greet, 0)

    spots = me * width + lax.broadcasted_iota(jnp.int32, live_ref.shape, 1)
    limit = blocks * width - docs_ref[0, docs_ref.shape[1] - 1]
    live_ref[...] = (spots < limit).astype(jnp.float32)
    layers = jnp.full(scale_ref.shape, layers_ref[section], jnp.int32)
    scale_ref[...] = 1.0 / jnp.sqrt(layers.astype(jnp.float32))
    live = live_ref[:1, :][None]
    scale = scale_ref[:1, :][None]
    prod_out[...] = (
        key_ref[...].astype(jnp.float32) * input_ref[...].astype(jnp.float32) * live
    ).astype(jnp.bfloat16)
    pl.semaphore_wait(barrier, blocks + 1)

    for pair in range(pairs):
        relay(pair).start()
    scatter(filter_ref, filter_wide, whole, FILTER)
    scatter(prod_out, prod_wide, whole, PRODUCT)
    settle(filter_wide, whole, FILTER).wait_recv()
    transform(filter_wide, filter_spec, range(pairs), spread_ref, ahead_ref, turns_ref)
    settle(prod_wide, whole, PRODUCT).wait_recv()
    transform(prod_wide, prod_spec, range(pairs), spread_ref, ahead_ref, turns_ref)
    multiply(
        filter_spec, prod_spec, False, conv_wide, range(pairs), gather_ref, back_ref, turns_ref
    )
    scatter(conv_wide, conv_ref, whole, CONV)

    for pair in range(pairs):
        span = part(pair)
        relay(pair).wait_recv()
        grad_out[:, span, :] = (
            scale
            * gate_ref[:, span, :].astype(jnp.float32)
            * incoming_ref[:, span, :].astype(jnp.float32)
        ).astype(jnp.bfloat16)
        scatter(grad_out, grad_wide, span, GRAD + pair)
        settle(grad_wide, span, GRAD + pair).wait_recv()
        transform(grad_wide, grad_spec, [pair], spread_ref, ahead_ref, turns_ref)
        multiply(
            filter_spec, grad_spec, True, corr_wide, [pair], gather_ref, back_ref, turns_ref
        )
        scatter(corr_wide, corr_ref, span, CORR + pair)
        multiply(prod_spec, grad_spec, True, lag_wide, [pair], gather_ref, back_ref, turns_ref)
        scatter(lag_wide, lag_ref, span, LAG + pair)

    settle(conv_ref, whole, CONV).wait_recv()
    settle(filter_wide, whole, FILTER).wait_send()
    settle(prod_wide, whole, PRODUCT).wait_send()
    settle(conv_ref, whole, CONV).wait_send()
    for pair in range(pairs):
        relay(pair).wait_send()
        settle(grad_wide, part(pair), GRAD + pair).wait_send()
        settle(corr_ref, part(pair), CORR + pair).wait()
        settle(lag_ref, part(pair), LAG + pair).wait()


def mixer(docs, layers, handed, gate, key, inputs, filters):
    blocks, channels, width = key.shape
    moved = jax.ShapeDtypeStruct(key.shape, jnp.bfloat16)
    line = jax.ShapeDtypeStruct((8, width), jnp.float32)
    wide = pltpu.VMEM(key.shape, jnp.bfloat16)
    spec = pltpu.VMEM((channels // GROUP, blocks * GROUP, 2 * width), jnp.float32)
    held = pl.BlockSpec(memory_space=pltpu.VMEM)
    small = pl.BlockSpec(memory_space=pltpu.SMEM)
    return pl.pallas_call(
        kernel,
        out_shape=(moved, moved, moved, moved, line, line),
        in_specs=[small] * 2 + [held] * 10,
        out_specs=(held,) * 6,
        scratch_shapes=[wide] * 8
        + [spec] * 3
        + [
            pltpu.SemaphoreType.DMA((STREAMS,)),
            pltpu.SemaphoreType.DMA((STREAMS,)),
            pltpu.SemaphoreType.DMA((2,)),
            pltpu.SemaphoreType.DMA((2,)),
        ],
        compiler_params=pltpu.CompilerParams(
            collective_id=0, has_side_effects=True, vmem_limit_bytes=40 * 1024 * 1024
        ),
    )(docs, layers, handed, gate, key, inputs, filters, *tables(blocks, width))


def body(handed_back, gate_q, key_k, input_x, filter_h, doc_lengths, section_layers):
    channels, width = gate_q.shape[2:]
    blocks = lax.axis_size("ctx")
    shape = (blocks, channels // blocks, width)
    blocked = [v.reshape(shape) for v in (handed_back, gate_q, key_k, input_x, filter_h)]
    incoming, conv, corr, lags, live, scale = mixer(doc_lengths, section_layers, *blocked)
    live, scale = live[0], scale[0]
    key32 = blocked[2].astype(jnp.float32)
    input32 = blocked[3].astype(jnp.float32)
    grad32 = incoming.astype(jnp.float32)
    corr32 = corr.astype(jnp.float32)
    grad_gate = (scale * grad32 * conv.astype(jnp.float32)).astype(jnp.bfloat16)
    grad_key = (corr32 * input32 * live).astype(jnp.bfloat16)
    grad_input = (grad32 + corr32 * key32 * live).astype(jnp.bfloat16)
    grad_filter = lags.astype(jnp.float32) / math.sqrt(blocks * width)
    flat = gate_q.shape
    return (
        grad_input.reshape(flat),
        grad_gate.reshape(flat),
        grad_key.reshape(flat),
        grad_filter.reshape(filter_h.shape),
    )


def solution(mesh):
    return jax.shard_map(
        body,
        mesh=mesh,
        in_specs=(
            P("pipe", None, "chan", "ctx"),
            P("pipe", None, "chan", "ctx"),
            P("pipe", None, "chan", "ctx"),
            P("pipe", None, "chan", "ctx"),
            P("pipe", "chan", "ctx"),
            P(),
            P(),
        ),
        out_specs=(
            P("pipe", None, "chan", "ctx"),
            P("pipe", None, "chan", "ctx"),
            P("pipe", None, "chan", "ctx"),
            P("pipe", "chan", "ctx"),
        ),
        check_vma=False,
    )
```

```python
import functools
import math

import jax
import jax.numpy as jnp
import numpy as np
from jax import lax
from jax.experimental import pallas as pl
from jax.experimental.pallas import tpu as pltpu
from jax.sharding import PartitionSpec as P

GROUP = 8


def halves(table):
    top = table.astype(jnp.bfloat16)
    rest = (table - top.astype(np.float64)).astype(jnp.bfloat16)
    return np.stack([top, rest])


@functools.lru_cache(maxsize=None)
def tables(blocks, width):
    length = blocks * width
    turn = 2.0 * math.pi
    row = np.arange(blocks)[:, None]
    quarter = np.arange(blocks)[:, None] + 0.25
    outer = turn * quarter * row.T / blocks
    wave = np.concatenate([np.cos(outer), -np.sin(outer)])
    spread = np.kron(wave, np.eye(GROUP))
    twist = np.repeat(turn * quarter * np.arange(width)[None, :] / length, GROUP, axis=0)
    lane = np.arange(width)
    inner = turn * ((lane[:, None] * lane[None, :]) % width) / width
    cos, sin = np.cos(inner), np.sin(inner)
    ahead = np.block([[cos, -sin], [sin, cos]])
    back = np.block([[cos, sin], [-sin, cos]])
    turns = np.stack([np.cos(twist), -np.sin(twist)]).astype(np.float32)
    return (halves(spread), halves(spread.T / length), halves(ahead), halves(back), turns)


def fixed_left(table_ref, right):
    return jnp.dot(table_ref[0], right, preferred_element_type=jnp.float32) + jnp.dot(
        table_ref[1], right, preferred_element_type=jnp.float32
    )


def fixed_right(left, table_ref):
    return jnp.dot(left, table_ref[0], preferred_element_type=jnp.float32) + jnp.dot(
        left, table_ref[1], preferred_element_type=jnp.float32
    )


def transform(wide_ref, spec_ref, pairs, spread_ref, ahead_ref, turns_ref):
    blocks, channels, width = wide_ref.shape
    rows = blocks * GROUP
    for pair in pairs:
        chunk = wide_ref[:, 2 * GROUP * pair : 2 * GROUP * (pair + 1), :].astype(jnp.float32)
        sides = [chunk[:, :GROUP, :].reshape(rows, width), chunk[:, GROUP:, :].reshape(rows, width)]
        mixed = fixed_left(spread_ref, jnp.concatenate(sides, axis=1).astype(jnp.bfloat16))
        for side in range(2):
            part = mixed[:, side * width : (side + 1) * width]
            part_re, part_im = part[:rows], part[rows:]
            turned = jnp.concatenate(
                [
                    part_re * turns_ref[0] - part_im * turns_ref[1],
                    part_re * turns_ref[1] + part_im * turns_ref[0],
                ],
                axis=1,
            )
            spec_ref[2 * pair + side] = fixed_right(turned.astype(jnp.bfloat16), ahead_ref)


def multiply(left_ref, right_ref, conjugate, wide_ref, pairs, gather_ref, back_ref, turns_ref):
    blocks, channels, width = wide_ref.shape
    rows = blocks * GROUP
    for pair in pairs:
        sides = []
        for side in range(2):
            left, right = left_ref[2 * pair + side], right_ref[2 * pair + side]
            left_re, left_im = left[:, :width], left[:, width:]
            right_re, right_im = right[:, :width], right[:, width:]
            if conjugate:
                left_im = -left_im
            both = jnp.concatenate(
                [left_re * right_re - left_im * right_im, left_re * right_im + left_im * right_re],
                axis=1,
            )
            part = fixed_right(both.astype(jnp.bfloat16), back_ref)
            part_re, part_im = part[:, :width], part[:, width:]
            sides.append(
                jnp.concatenate(
                    [
                        part_re * turns_ref[0] + part_im * turns_ref[1],
                        part_im * turns_ref[0] - part_re * turns_ref[1],
                    ],
                    axis=0,
                )
            )
        signal = fixed_left(gather_ref, jnp.concatenate(sides, axis=1).astype(jnp.bfloat16))
        outs = [signal[:, s * width : (s + 1) * width].reshape(blocks, GROUP, width) for s in range(2)]
        chunk = jnp.concatenate(outs, axis=1).astype(jnp.bfloat16)
        wide_ref[:, 2 * GROUP * pair : 2 * GROUP * (pair + 1), :] = chunk

MESH = pl.DeviceIdType.MESH
FILTER, PRODUCT, CONV, GRAD, CORR, LAG = 0, 1, 2, 3, 5, 7
STREAMS = 9


def kernel(
    docs_ref, layers_ref, handed_ref, gate_home, key_home, input_home, filter_ref,
    spread_home, gather_home, ahead_home, back_home, turns_home,
    incoming_ref, conv_ref, corr_ref, lag_ref, live_ref, scale_ref,
    prod_out, grad_out, filter_wide, prod_wide, grad_wide, conv_wide, corr_wide, lag_wide,
    filter_spec, prod_spec, grad_spec,
    gate_ref, key_ref, input_ref, spread_ref, gather_ref, ahead_ref, back_ref, turns_ref,
    send_sems, recv_sems, relay_send, relay_recv, load_sems,
):
    blocks, channels, width = key_ref.shape
    me = lax.axis_index("ctx")
    section, sections = lax.axis_index("pipe"), lax.axis_size("pipe")
    before = lax.rem(section + sections - 1, sections)
    after = lax.rem(section + 1, sections)
    pairs = channels // (2 * GROUP)
    whole = pl.ds(0, channels)

    def part(pair):
        return pl.ds(2 * GROUP * pair, 2 * GROUP)

    def relay(pair):
        return pltpu.make_async_remote_copy(
            src_ref=handed_ref.at[:, part(pair), :],
            dst_ref=incoming_ref.at[:, part(pair), :],
            send_sem=relay_send.at[pair],
            recv_sem=relay_recv.at[pair],
            device_id={"pipe": before},
            device_id_type=MESH,
        )

    def scatter(source, target, span, stream):
        def step(index, carry):
            peer = lax.rem(me + index, blocks)
            pltpu.make_async_remote_copy(
                src_ref=source.at[peer, span, :],
                dst_ref=target.at[me, span, :],
                send_sem=send_sems.at[stream],
                recv_sem=recv_sems.at[stream],
                device_id={"ctx": peer},
                device_id_type=MESH,
            ).start()
            return carry

        lax.fori_loop(1, blocks, step, 0)

    def settle(buffer, span, stream):
        others = buffer.at[pl.ds(0, blocks - 1), span, :]
        return pltpu.make_async_remote_copy(
            src_ref=others,
            dst_ref=others,
            send_sem=send_sems.at[stream],
            recv_sem=recv_sems.at[stream],
            device_id={"ctx": lax.rem(me + 1, blocks)},
            device_id_type=MESH,
        )

    def keep(source, target, span):
        target[me, span, :] = source[me, span, :]

    loads = [
        pltpu.make_async_copy(source, target, load_sems.at[index])
        for index, (source, target) in enumerate(
            [
                (key_home, key_ref),
                (input_home, input_ref),
                (spread_home, spread_ref),
                (ahead_home, ahead_ref),
                (turns_home, turns_ref),
                (back_home, back_ref),
                (gather_home, gather_ref),
                (gate_home, gate_ref),
                (filter_ref.at[me], filter_wide.at[me]),
            ]
        )
    ]
    barrier = pltpu.get_barrier_semaphore()

    def greet(index, carry):
        pl.semaphore_signal(
            barrier, inc=1, device_id={"ctx": lax.rem(me + index, blocks)}, device_id_type=MESH
        )
        return carry

    for neighbour in (before, after):
        pl.semaphore_signal(barrier, inc=1, device_id={"pipe": neighbour}, device_id_type=MESH)
    lax.fori_loop(1, blocks, greet, 0)
    for load in loads:
        load.start()

    spots = me * width + lax.broadcasted_iota(jnp.int32, live_ref.shape, 1)
    limit = blocks * width - docs_ref[0, docs_ref.shape[1] - 1]
    live_ref[...] = (spots < limit).astype(jnp.float32)
    layers = jnp.full(scale_ref.shape, layers_ref[section], jnp.int32)
    scale_ref[...] = 1.0 / jnp.sqrt(layers.astype(jnp.float32))
    live = live_ref[:1, :][None]
    scale = scale_ref[:1, :][None]
    loads[0].wait()
    loads[1].wait()
    prod_out[...] = (
        key_ref[...].astype(jnp.float32) * input_ref[...].astype(jnp.float32) * live
    ).astype(jnp.bfloat16)
    pl.semaphore_wait(barrier, blocks + 1)

    for pair in range(pairs):
        relay(pair).start()
    scatter(filter_ref, filter_wide, whole, FILTER)
    scatter(prod_out, prod_wide, whole, PRODUCT)
    keep(prod_out, prod_wide, whole)
    for load in loads[2:]:
        load.wait()
    settle(filter_wide, whole, FILTER).wait_recv()
    transform(filter_wide, filter_spec, range(pairs), spread_ref, ahead_ref, turns_ref)
    settle(prod_wide, whole, PRODUCT).wait_recv()
    transform(prod_wide, prod_spec, range(pairs), spread_ref, ahead_ref, turns_ref)
    multiply(
        filter_spec, prod_spec, False, conv_wide, range(pairs), gather_ref, back_ref, turns_ref
    )
    scatter(conv_wide, conv_ref, whole, CONV)
    keep(conv_wide, conv_ref, whole)

    for pair in range(pairs):
        span = part(pair)
        relay(pair).wait_recv()
        grad_out[:, span, :] = (
            scale
            * gate_ref[:, span, :].astype(jnp.float32)
            * incoming_ref[:, span, :].astype(jnp.float32)
        ).astype(jnp.bfloat16)
        scatter(grad_out, grad_wide, span, GRAD + pair)
        keep(grad_out, grad_wide, span)
        settle(grad_wide, span, GRAD + pair).wait_recv()
        transform(grad_wide, grad_spec, [pair], spread_ref, ahead_ref, turns_ref)
        multiply(
            filter_spec, grad_spec, True, corr_wide, [pair], gather_ref, back_ref, turns_ref
        )
        scatter(corr_wide, corr_ref, span, CORR + pair)
        keep(corr_wide, corr_ref, span)
        multiply(prod_spec, grad_spec, True, lag_wide, [pair], gather_ref, back_ref, turns_ref)
        scatter(lag_wide, lag_ref, span, LAG + pair)
        keep(lag_wide, lag_ref, span)

    settle(conv_ref, whole, CONV).wait_recv()
    settle(filter_wide, whole, FILTER).wait_send()
    settle(prod_wide, whole, PRODUCT).wait_send()
    settle(conv_ref, whole, CONV).wait_send()
    for pair in range(pairs):
        relay(pair).wait_send()
        settle(grad_wide, part(pair), GRAD + pair).wait_send()
        settle(corr_ref, part(pair), CORR + pair).wait()
        settle(lag_ref, part(pair), LAG + pair).wait()


def mixer(docs, layers, handed, gate, key, inputs, filters):
    blocks, channels, width = key.shape
    moved = jax.ShapeDtypeStruct(key.shape, jnp.bfloat16)
    line = jax.ShapeDtypeStruct((8, width), jnp.float32)
    wide = pltpu.VMEM(key.shape, jnp.bfloat16)
    spec = pltpu.VMEM((channels // GROUP, blocks * GROUP, 2 * width), jnp.float32)
    held = pl.BlockSpec(memory_space=pltpu.VMEM)
    small = pl.BlockSpec(memory_space=pltpu.SMEM)
    far = pl.BlockSpec(memory_space=pl.ANY)
    fixed = tables(blocks, width)
    return pl.pallas_call(
        kernel,
        out_shape=(moved, moved, moved, moved, line, line),
        in_specs=[small] * 2 + [far] * 10,
        out_specs=(held,) * 6,
        scratch_shapes=[wide] * 8
        + [spec] * 3
        + [wide] * 3
        + [pltpu.VMEM(table.shape, table.dtype) for table in fixed]
        + [
            pltpu.SemaphoreType.DMA((STREAMS,)),
            pltpu.SemaphoreType.DMA((STREAMS,)),
            pltpu.SemaphoreType.DMA((2,)),
            pltpu.SemaphoreType.DMA((2,)),
            pltpu.SemaphoreType.DMA((9,)),
        ],
        compiler_params=pltpu.CompilerParams(
            collective_id=0, has_side_effects=True, vmem_limit_bytes=60 * 1024 * 1024
        ),
    )(docs, layers, handed, gate, key, inputs, filters, *fixed)


def body(handed_back, gate_q, key_k, input_x, filter_h, doc_lengths, section_layers):
    channels, width = gate_q.shape[2:]
    blocks = lax.axis_size("ctx")
    shape = (blocks, channels // blocks, width)
    blocked = [v.reshape(shape) for v in (handed_back, gate_q, key_k, input_x, filter_h)]
    incoming, conv, corr, lags, live, scale = mixer(doc_lengths, section_layers, *blocked)
    live, scale = live[0], scale[0]
    key32 = blocked[2].astype(jnp.float32)
    input32 = blocked[3].astype(jnp.float32)
    grad32 = incoming.astype(jnp.float32)
    corr32 = corr.astype(jnp.float32)
    grad_gate = (scale * grad32 * conv.astype(jnp.float32)).astype(jnp.bfloat16)
    grad_key = (corr32 * input32 * live).astype(jnp.bfloat16)
    grad_input = (grad32 + corr32 * key32 * live).astype(jnp.bfloat16)
    grad_filter = lags.astype(jnp.float32) / math.sqrt(blocks * width)
    flat = gate_q.shape
    return (
        grad_input.reshape(flat),
        grad_gate.reshape(flat),
        grad_key.reshape(flat),
        grad_filter.reshape(filter_h.shape),
    )


def solution(mesh):
    return jax.shard_map(
        body,
        mesh=mesh,
        in_specs=(
            P("pipe", None, "chan", "ctx"),
            P("pipe", None, "chan", "ctx"),
            P("pipe", None, "chan", "ctx"),
            P("pipe", None, "chan", "ctx"),
            P("pipe", "chan", "ctx"),
            P(),
            P(),
        ),
        out_specs=(
            P("pipe", None, "chan", "ctx"),
            P("pipe", None, "chan", "ctx"),
            P("pipe", None, "chan", "ctx"),
            P("pipe", "chan", "ctx"),
        ),
        check_vma=False,
    )
```

```python
import functools
import math

import jax
import jax.numpy as jnp
import numpy as np
from jax import lax
from jax.experimental import pallas as pl
from jax.experimental.pallas import tpu as pltpu
from jax.sharding import PartitionSpec as P

GROUP = 8


def halves(table):
    top = table.astype(jnp.bfloat16)
    rest = (table - top.astype(np.float64)).astype(jnp.bfloat16)
    return np.stack([top, rest])


@functools.lru_cache(maxsize=None)
def tables(blocks, width):
    length = blocks * width
    turn = 2.0 * math.pi
    row = np.arange(blocks)[:, None]
    quarter = np.arange(blocks)[:, None] + 0.25
    outer = turn * quarter * row.T / blocks
    wave = np.concatenate([np.cos(outer), -np.sin(outer)])
    spread = np.kron(wave, np.eye(GROUP))
    twist = np.repeat(turn * quarter * np.arange(width)[None, :] / length, GROUP, axis=0)
    lane = np.arange(width)
    inner = turn * ((lane[:, None] * lane[None, :]) % width) / width
    cos, sin = np.cos(inner), np.sin(inner)
    ahead = np.block([[cos, -sin], [sin, cos]])
    back = np.block([[cos, sin], [-sin, cos]])
    turns = np.stack([np.cos(twist), -np.sin(twist)]).astype(np.float32)
    return (halves(spread), halves(spread.T / length), halves(ahead), halves(back), turns)


def fixed_left(table_ref, right):
    return jnp.dot(table_ref[0], right, preferred_element_type=jnp.float32) + jnp.dot(
        table_ref[1], right, preferred_element_type=jnp.float32
    )


def fixed_right(left, table_ref):
    return jnp.dot(left, table_ref[0], preferred_element_type=jnp.float32) + jnp.dot(
        left, table_ref[1], preferred_element_type=jnp.float32
    )


def transform(wide_ref, spec_ref, span, spread_ref, ahead_ref, turns_ref):
    blocks, channels, width = wide_ref.shape
    rows = blocks * GROUP
    first, count = span
    for start in range(first, first + count, 2):
        groups = range(start, min(start + 2, first + count))
        chunk = wide_ref[:, GROUP * start : GROUP * (groups[-1] + 1), :].astype(jnp.float32)
        sides = [
            chunk[:, GROUP * (g - start) : GROUP * (g - start + 1), :].reshape(rows, width)
            for g in groups
        ]
        mixed = fixed_left(spread_ref, jnp.concatenate(sides, axis=1).astype(jnp.bfloat16))
        for side, group in enumerate(groups):
            part = mixed[:, side * width : (side + 1) * width]
            part_re, part_im = part[:rows], part[rows:]
            turned = jnp.concatenate(
                [
                    part_re * turns_ref[0] - part_im * turns_ref[1],
                    part_re * turns_ref[1] + part_im * turns_ref[0],
                ],
                axis=1,
            )
            spec_ref[group] = fixed_right(turned.astype(jnp.bfloat16), ahead_ref)


def multiply(left_ref, right_ref, conjugate, wide_ref, span, gather_ref, back_ref, turns_ref):
    blocks, channels, width = wide_ref.shape
    first, count = span
    for start in range(first, first + count, 2):
        groups = range(start, min(start + 2, first + count))
        sides = []
        for group in groups:
            left, right = left_ref[group], right_ref[group]
            left_re, left_im = left[:, :width], left[:, width:]
            right_re, right_im = right[:, :width], right[:, width:]
            if conjugate:
                left_im = -left_im
            both = jnp.concatenate(
                [left_re * right_re - left_im * right_im, left_re * right_im + left_im * right_re],
                axis=1,
            )
            part = fixed_right(both.astype(jnp.bfloat16), back_ref)
            part_re, part_im = part[:, :width], part[:, width:]
            sides.append(
                jnp.concatenate(
                    [
                        part_re * turns_ref[0] + part_im * turns_ref[1],
                        part_im * turns_ref[0] - part_re * turns_ref[1],
                    ],
                    axis=0,
                )
            )
        signal = fixed_left(gather_ref, jnp.concatenate(sides, axis=1).astype(jnp.bfloat16))
        outs = [
            signal[:, s * width : (s + 1) * width].reshape(blocks, GROUP, width)
            for s in range(len(sides))
        ]
        chunk = jnp.concatenate(outs, axis=1).astype(jnp.bfloat16)
        wide_ref[:, GROUP * start : GROUP * (groups[-1] + 1), :] = chunk


MESH = pl.DeviceIdType.MESH
FILTER, PRODUCT, CONV, GRAD, CORR, LAG = 0, 1, 2, 3, 6, 9
STREAMS = 12


def kernel(
    docs_ref, layers_ref, handed_ref, gate_home, key_home, input_home, filter_ref,
    spread_home, gather_home, ahead_home, back_home, turns_home,
    incoming_ref, conv_ref, corr_ref, lag_ref, live_ref, scale_ref,
    prod_out, grad_out, filter_wide, prod_wide, grad_wide, conv_wide, corr_wide, lag_wide,
    filter_spec, prod_spec, grad_spec,
    gate_ref, key_ref, input_ref, spread_ref, gather_ref, ahead_ref, back_ref, turns_ref,
    send_sems, recv_sems, relay_send, relay_recv, load_sems,
):
    blocks, channels, width = key_ref.shape
    me = lax.axis_index("ctx")
    section, sections = lax.axis_index("pipe"), lax.axis_size("pipe")
    before = lax.rem(section + sections - 1, sections)
    after = lax.rem(section + 1, sections)
    groups = channels // GROUP
    whole, every = pl.ds(0, channels), (0, groups)
    quarter = groups // 4
    pieces = [(0, groups - 2 * quarter), (groups - 2 * quarter, quarter), (groups - quarter, quarter)]

    def part(piece):
        first, count = pieces[piece]
        return pl.ds(GROUP * first, GROUP * count)

    def relay(piece):
        return pltpu.make_async_remote_copy(
            src_ref=handed_ref.at[:, part(piece), :],
            dst_ref=incoming_ref.at[:, part(piece), :],
            send_sem=relay_send.at[piece],
            recv_sem=relay_recv.at[piece],
            device_id={"pipe": before},
            device_id_type=MESH,
        )

    def scatter(source, target, span, stream):
        def step(index, carry):
            peer = lax.rem(me + index, blocks)
            pltpu.make_async_remote_copy(
                src_ref=source.at[peer, span, :],
                dst_ref=target.at[me, span, :],
                send_sem=send_sems.at[stream],
                recv_sem=recv_sems.at[stream],
                device_id={"ctx": peer},
                device_id_type=MESH,
            ).start()
            return carry

        lax.fori_loop(1, blocks, step, 0)

    def settle(buffer, span, stream):
        others = buffer.at[pl.ds(0, blocks - 1), span, :]
        return pltpu.make_async_remote_copy(
            src_ref=others,
            dst_ref=others,
            send_sem=send_sems.at[stream],
            recv_sem=recv_sems.at[stream],
            device_id={"ctx": lax.rem(me + 1, blocks)},
            device_id_type=MESH,
        )

    def keep(source, target, span):
        target[me, span, :] = source[me, span, :]

    loads = [
        pltpu.make_async_copy(source, target, load_sems.at[index])
        for index, (source, target) in enumerate(
            [
                (key_home, key_ref),
                (input_home, input_ref),
                (spread_home, spread_ref),
                (ahead_home, ahead_ref),
                (turns_home, turns_ref),
                (back_home, back_ref),
                (gather_home, gather_ref),
                (gate_home, gate_ref),
                (filter_ref.at[me], filter_wide.at[me]),
            ]
        )
    ]
    barrier = pltpu.get_barrier_semaphore()

    def greet(index, carry):
        pl.semaphore_signal(
            barrier, inc=1, device_id={"ctx": lax.rem(me + index, blocks)}, device_id_type=MESH
        )
        return carry

    for neighbour in (before, after):
        pl.semaphore_signal(barrier, inc=1, device_id={"pipe": neighbour}, device_id_type=MESH)
    lax.fori_loop(1, blocks, greet, 0)
    for load in loads:
        load.start()

    spots = me * width + lax.broadcasted_iota(jnp.int32, live_ref.shape, 1)
    limit = blocks * width - docs_ref[0, docs_ref.shape[1] - 1]
    live_ref[...] = (spots < limit).astype(jnp.float32)
    layers = jnp.full(scale_ref.shape, layers_ref[section], jnp.int32)
    scale_ref[...] = 1.0 / jnp.sqrt(layers.astype(jnp.float32))
    live = live_ref[...][None]
    scale = scale_ref[...][None]
    loads[0].wait()
    loads[1].wait()
    prod_out[...] = (
        key_ref[...].astype(jnp.float32) * input_ref[...].astype(jnp.float32) * live
    ).astype(jnp.bfloat16)
    pl.semaphore_wait(barrier, blocks + 1)

    for piece in range(len(pieces)):
        relay(piece).start()
    scatter(filter_ref, filter_wide, whole, FILTER)
    scatter(prod_out, prod_wide, whole, PRODUCT)
    keep(prod_out, prod_wide, whole)
    for load in loads[2:]:
        load.wait()
    settle(filter_wide, whole, FILTER).wait_recv()
    transform(filter_wide, filter_spec, every, spread_ref, ahead_ref, turns_ref)
    settle(prod_wide, whole, PRODUCT).wait_recv()
    transform(prod_wide, prod_spec, every, spread_ref, ahead_ref, turns_ref)
    multiply(
        filter_spec, prod_spec, False, conv_wide, every, gather_ref, back_ref, turns_ref
    )
    scatter(conv_wide, conv_ref, whole, CONV)
    keep(conv_wide, conv_ref, whole)

    for piece in range(len(pieces)):
        span = part(piece)
        relay(piece).wait_recv()
        grad_out[:, span, :] = (
            scale
            * gate_ref[:, span, :].astype(jnp.float32)
            * incoming_ref[:, span, :].astype(jnp.float32)
        ).astype(jnp.bfloat16)
        scatter(grad_out, grad_wide, span, GRAD + piece)
        keep(grad_out, grad_wide, span)
        settle(grad_wide, span, GRAD + piece).wait_recv()
        transform(grad_wide, grad_spec, pieces[piece], spread_ref, ahead_ref, turns_ref)
        multiply(
            filter_spec, grad_spec, True, corr_wide, pieces[piece], gather_ref, back_ref, turns_ref
        )
        scatter(corr_wide, corr_ref, span, CORR + piece)
        keep(corr_wide, corr_ref, span)
        multiply(prod_spec, grad_spec, True, lag_wide, pieces[piece], gather_ref, back_ref, turns_ref)
        scatter(lag_wide, lag_ref, span, LAG + piece)
        keep(lag_wide, lag_ref, span)

    settle(conv_ref, whole, CONV).wait_recv()
    settle(filter_wide, whole, FILTER).wait_send()
    settle(prod_wide, whole, PRODUCT).wait_send()
    settle(conv_ref, whole, CONV).wait_send()
    for piece in range(len(pieces)):
        relay(piece).wait_send()
        settle(grad_wide, part(piece), GRAD + piece).wait_send()
        settle(corr_ref, part(piece), CORR + piece).wait()
        settle(lag_ref, part(piece), LAG + piece).wait()


def mixer(docs, layers, handed, gate, key, inputs, filters):
    blocks, channels, width = key.shape
    moved = jax.ShapeDtypeStruct(key.shape, jnp.bfloat16)
    line = jax.ShapeDtypeStruct((1, width), jnp.float32)
    wide = pltpu.VMEM(key.shape, jnp.bfloat16)
    spec = pltpu.VMEM((channels // GROUP, blocks * GROUP, 2 * width), jnp.float32)
    held = pl.BlockSpec(memory_space=pltpu.VMEM)
    small = pl.BlockSpec(memory_space=pltpu.SMEM)
    far = pl.BlockSpec(memory_space=pl.ANY)
    fixed = tables(blocks, width)
    return pl.pallas_call(
        kernel,
        out_shape=(moved, moved, moved, moved, line, line),
        in_specs=[small] * 2 + [far] * 10,
        out_specs=(held,) * 6,
        scratch_shapes=[wide] * 8
        + [spec] * 3
        + [wide] * 3
        + [pltpu.VMEM(table.shape, table.dtype) for table in fixed]
        + [
            pltpu.SemaphoreType.DMA((STREAMS,)),
            pltpu.SemaphoreType.DMA((STREAMS,)),
            pltpu.SemaphoreType.DMA((3,)),
            pltpu.SemaphoreType.DMA((3,)),
            pltpu.SemaphoreType.DMA((9,)),
        ],
        compiler_params=pltpu.CompilerParams(
            collective_id=0, has_side_effects=True, vmem_limit_bytes=60 * 1024 * 1024
        ),
    )(docs, layers, handed, gate, key, inputs, filters, *fixed)


def body(handed_back, gate_q, key_k, input_x, filter_h, doc_lengths, section_layers):
    channels, width = gate_q.shape[2:]
    blocks = lax.axis_size("ctx")
    shape = (blocks, channels // blocks, width)
    blocked = [v.reshape(shape) for v in (handed_back, gate_q, key_k, input_x, filter_h)]
    incoming, conv, corr, lags, live, scale = mixer(doc_lengths, section_layers, *blocked)
    live, scale = live[None], scale[None]
    key32 = blocked[2].astype(jnp.float32)
    input32 = blocked[3].astype(jnp.float32)
    grad32 = incoming.astype(jnp.float32)
    corr32 = corr.astype(jnp.float32)
    grad_gate = (scale * grad32 * conv.astype(jnp.float32)).astype(jnp.bfloat16)
    grad_key = (corr32 * input32 * live).astype(jnp.bfloat16)
    grad_input = (grad32 + corr32 * key32 * live).astype(jnp.bfloat16)
    grad_filter = lags.astype(jnp.float32) / math.sqrt(blocks * width)
    flat = gate_q.shape
    return (
        grad_input.reshape(flat),
        grad_gate.reshape(flat),
        grad_key.reshape(flat),
        grad_filter.reshape(filter_h.shape),
    )


def solution(mesh):
    return jax.shard_map(
        body,
        mesh=mesh,
        in_specs=(
            P("pipe", None, "chan", "ctx"),
            P("pipe", None, "chan", "ctx"),
            P("pipe", None, "chan", "ctx"),
            P("pipe", None, "chan", "ctx"),
            P("pipe", "chan", "ctx"),
            P(),
            P(),
        ),
        out_specs=(
            P("pipe", None, "chan", "ctx"),
            P("pipe", None, "chan", "ctx"),
            P("pipe", None, "chan", "ctx"),
            P("pipe", "chan", "ctx"),
        ),
        check_vma=False,
    )
```

```python
import functools
import math

import jax
import jax.numpy as jnp
import numpy as np
from jax import lax
from jax.experimental import pallas as pl
from jax.experimental.pallas import tpu as pltpu
from jax.sharding import PartitionSpec as P

GROUP = 8


def halves(table):
    top = table.astype(jnp.bfloat16)
    rest = (table - top.astype(np.float64)).astype(jnp.bfloat16)
    return np.stack([top, rest])


@functools.lru_cache(maxsize=None)
def tables(blocks, width):
    length = blocks * width
    turn = 2.0 * math.pi
    row = np.arange(blocks)[:, None]
    quarter = np.arange(blocks)[:, None] + 0.25
    outer = turn * quarter * row.T / blocks
    wave = np.concatenate([np.cos(outer), -np.sin(outer)])
    spread = np.kron(wave, np.eye(GROUP))
    twist = np.repeat(turn * quarter * np.arange(width)[None, :] / length, GROUP, axis=0)
    lane = np.arange(width)
    inner = turn * ((lane[:, None] * lane[None, :]) % width) / width
    cos, sin = np.cos(inner), np.sin(inner)
    ahead = np.block([[cos, -sin], [sin, cos]])
    back = np.block([[cos, sin], [-sin, cos]])
    turns = np.stack([np.cos(twist), -np.sin(twist)]).astype(np.float32)
    return (halves(spread), halves(spread.T / length), halves(ahead), halves(back), turns)


def fixed_left(table_ref, right):
    return jnp.dot(table_ref[0], right, preferred_element_type=jnp.float32) + jnp.dot(
        table_ref[1], right, preferred_element_type=jnp.float32
    )


def fixed_right(left, table_ref):
    return jnp.dot(left, table_ref[0], preferred_element_type=jnp.float32) + jnp.dot(
        left, table_ref[1], preferred_element_type=jnp.float32
    )


def transform(wide_ref, spec_ref, span, spread_ref, ahead_ref, turns_ref):
    blocks, channels, width = wide_ref.shape
    rows = blocks * GROUP
    first, count = span
    for start in range(first, first + count, 2):
        groups = range(start, min(start + 2, first + count))
        chunk = wide_ref[:, GROUP * start : GROUP * (groups[-1] + 1), :].astype(jnp.float32)
        sides = [
            chunk[:, GROUP * (g - start) : GROUP * (g - start + 1), :].reshape(rows, width)
            for g in groups
        ]
        mixed = fixed_left(spread_ref, jnp.concatenate(sides, axis=1).astype(jnp.bfloat16))
        for side, group in enumerate(groups):
            part = mixed[:, side * width : (side + 1) * width]
            part_re, part_im = part[:rows], part[rows:]
            turned = jnp.concatenate(
                [
                    part_re * turns_ref[0] - part_im * turns_ref[1],
                    part_re * turns_ref[1] + part_im * turns_ref[0],
                ],
                axis=1,
            )
            spec_ref[group] = fixed_right(turned.astype(jnp.bfloat16), ahead_ref)


def multiply(left_ref, right_ref, conjugate, wide_ref, span, gather_ref, back_ref, turns_ref):
    blocks, channels, width = wide_ref.shape
    first, count = span
    for start in range(first, first + count, 2):
        groups = range(start, min(start + 2, first + count))
        sides = []
        for group in groups:
            left, right = left_ref[group], right_ref[group]
            left_re, left_im = left[:, :width], left[:, width:]
            right_re, right_im = right[:, :width], right[:, width:]
            if conjugate:
                left_im = -left_im
            both = jnp.concatenate(
                [left_re * right_re - left_im * right_im, left_re * right_im + left_im * right_re],
                axis=1,
            )
            part = fixed_right(both.astype(jnp.bfloat16), back_ref)
            part_re, part_im = part[:, :width], part[:, width:]
            sides.append(
                jnp.concatenate(
                    [
                        part_re * turns_ref[0] + part_im * turns_ref[1],
                        part_im * turns_ref[0] - part_re * turns_ref[1],
                    ],
                    axis=0,
                )
            )
        signal = fixed_left(gather_ref, jnp.concatenate(sides, axis=1).astype(jnp.bfloat16))
        outs = [
            signal[:, s * width : (s + 1) * width].reshape(blocks, GROUP, width)
            for s in range(len(sides))
        ]
        chunk = jnp.concatenate(outs, axis=1).astype(jnp.bfloat16)
        wide_ref[:, GROUP * (start - first) : GROUP * (groups[-1] + 1 - first), :] = chunk


MESH = pl.DeviceIdType.MESH
PIECES = 2
OUTWARD, CONV, GRAD, BACK = 0, 1, 2, 2 + PIECES
STREAMS = 2 + 2 * PIECES
LOADS = 9


def kernel(
    docs_ref, layers_ref, handed_ref, gate_home, key_home, input_home, filter_ref,
    spread_home, gather_home, ahead_home, back_home, turns_home,
    incoming_ref, conv_ref, both_ref, live_ref, scale_ref,
    first_out, first_wide, grad_out, grad_wide, conv_wide, both_wide,
    filter_spec, prod_spec, grad_spec,
    gate_ref, key_ref, input_ref, spread_ref, gather_ref, ahead_ref, back_ref, turns_ref,
    send_sems, recv_sems, relay_send, relay_recv, load_sems,
):
    blocks, channels, width = key_ref.shape
    me = lax.axis_index("ctx")
    section, sections = lax.axis_index("pipe"), lax.axis_size("pipe")
    before = lax.rem(section + sections - 1, sections)
    after = lax.rem(section + 1, sections)
    share = channels // PIECES
    every = (0, channels // GROUP)

    def part(ref, piece):
        return ref.at[:, pl.ds(share * piece, share), :]

    def groups(piece):
        return (share * piece // GROUP, share // GROUP)

    def relay(piece):
        return pltpu.make_async_remote_copy(
            src_ref=part(handed_ref, piece),
            dst_ref=part(incoming_ref, piece),
            send_sem=relay_send.at[piece],
            recv_sem=relay_recv.at[piece],
            device_id={"pipe": before},
            device_id_type=MESH,
        )

    def scatter(source, target, stream):
        def step(index, carry):
            peer = lax.rem(me + index, blocks)
            pltpu.make_async_remote_copy(
                src_ref=source.at[peer],
                dst_ref=target.at[me],
                send_sem=send_sems.at[stream],
                recv_sem=recv_sems.at[stream],
                device_id={"ctx": peer},
                device_id_type=MESH,
            ).start()
            return carry

        lax.fori_loop(1, blocks, step, 0)
        target[me] = source[me]

    def settle(buffer, stream):
        others = buffer.at[pl.ds(0, blocks - 1)]
        return pltpu.make_async_remote_copy(
            src_ref=others,
            dst_ref=others,
            send_sem=send_sems.at[stream],
            recv_sem=recv_sems.at[stream],
            device_id={"ctx": lax.rem(me + 1, blocks)},
            device_id_type=MESH,
        )

    loads = [
        pltpu.make_async_copy(source, target, load_sems.at[index])
        for index, (source, target) in enumerate(
            [
                (key_home, key_ref),
                (input_home, input_ref),
                (filter_ref, first_out.at[:, 0]),
                (spread_home, spread_ref),
                (ahead_home, ahead_ref),
                (turns_home, turns_ref),
                (back_home, back_ref),
                (gather_home, gather_ref),
                (gate_home, gate_ref),
            ]
        )
    ]
    barrier = pltpu.get_barrier_semaphore()

    def greet(index, carry):
        pl.semaphore_signal(
            barrier, inc=1, device_id={"ctx": lax.rem(me + index, blocks)}, device_id_type=MESH
        )
        return carry

    for neighbour in (before, after):
        pl.semaphore_signal(barrier, inc=1, device_id={"pipe": neighbour}, device_id_type=MESH)
    lax.fori_loop(1, blocks, greet, 0)
    for load in loads:
        load.start()

    spots = me * width + lax.broadcasted_iota(jnp.int32, live_ref.shape, 1)
    limit = blocks * width - docs_ref[0, docs_ref.shape[1] - 1]
    live_ref[...] = (spots < limit).astype(jnp.float32)
    layers = jnp.full(scale_ref.shape, layers_ref[section], jnp.int32)
    scale_ref[...] = 1.0 / jnp.sqrt(layers.astype(jnp.float32))
    live = live_ref[...][None]
    scale = scale_ref[...][None]
    for load in loads[:3]:
        load.wait()
    first_out[:, 1] = (
        key_ref[...].astype(jnp.float32) * input_ref[...].astype(jnp.float32) * live
    ).astype(jnp.bfloat16)
    pl.semaphore_wait(barrier, blocks + 1)

    for piece in range(PIECES):
        relay(piece).start()
    scatter(first_out, first_wide, OUTWARD)
    for load in loads[3:]:
        load.wait()
    settle(first_wide, OUTWARD).wait_recv()
    transform(first_wide.at[:, 0], filter_spec, every, spread_ref, ahead_ref, turns_ref)
    transform(first_wide.at[:, 1], prod_spec, every, spread_ref, ahead_ref, turns_ref)
    multiply(filter_spec, prod_spec, False, conv_wide, every, gather_ref, back_ref, turns_ref)
    scatter(conv_wide, conv_ref, CONV)

    def send_grad(piece):
        relay(piece).wait_recv()
        span = pl.ds(share * piece, share)
        grad_out[:, span, :] = (
            scale
            * gate_ref[:, span, :].astype(jnp.float32)
            * incoming_ref[:, span, :].astype(jnp.float32)
        ).astype(jnp.bfloat16)
        scatter(part(grad_out, piece), part(grad_wide, piece), GRAD + piece)

    def send_back(piece):
        span = groups(piece)
        settle(part(grad_wide, piece), GRAD + piece).wait_recv()
        transform(grad_wide, grad_spec, span, spread_ref, ahead_ref, turns_ref)
        for index, spec in enumerate((filter_spec, prod_spec)):
            multiply(
                spec, grad_spec, True, both_wide.at[:, piece, index], span,
                gather_ref, back_ref, turns_ref,
            )
        scatter(both_wide.at[:, piece], both_ref.at[:, piece], BACK + piece)

    for piece in range(PIECES):
        send_grad(piece)
    for piece in range(PIECES):
        send_back(piece)

    settle(conv_ref, CONV).wait()
    settle(first_wide, OUTWARD).wait_send()
    for piece in range(PIECES):
        relay(piece).wait_send()
        settle(part(grad_wide, piece), GRAD + piece).wait_send()
        settle(both_ref.at[:, piece], BACK + piece).wait()


def mixer(docs, layers, handed, gate, key, inputs, filters):
    blocks, channels, width = key.shape
    moved = jax.ShapeDtypeStruct(key.shape, jnp.bfloat16)
    both = (blocks, PIECES, 2, channels // PIECES, width)
    line = jax.ShapeDtypeStruct((1, width), jnp.float32)
    wide = pltpu.VMEM(key.shape, jnp.bfloat16)
    double = pltpu.VMEM((blocks, 2, channels, width), jnp.bfloat16)
    spec = pltpu.VMEM((channels // GROUP, blocks * GROUP, 2 * width), jnp.float32)
    held = pl.BlockSpec(memory_space=pltpu.VMEM)
    small = pl.BlockSpec(memory_space=pltpu.SMEM)
    far = pl.BlockSpec(memory_space=pl.ANY)
    fixed = tables(blocks, width)
    return pl.pallas_call(
        kernel,
        out_shape=(moved, moved, jax.ShapeDtypeStruct(both, jnp.bfloat16), line, line),
        in_specs=[small] * 2 + [far] * 10,
        out_specs=(held,) * 5,
        scratch_shapes=[double, double, wide, wide, wide, pltpu.VMEM(both, jnp.bfloat16)]
        + [spec] * 3
        + [wide] * 3
        + [pltpu.VMEM(table.shape, table.dtype) for table in fixed]
        + [
            pltpu.SemaphoreType.DMA((STREAMS,)),
            pltpu.SemaphoreType.DMA((STREAMS,)),
            pltpu.SemaphoreType.DMA((PIECES,)),
            pltpu.SemaphoreType.DMA((PIECES,)),
            pltpu.SemaphoreType.DMA((LOADS,)),
        ],
        compiler_params=pltpu.CompilerParams(
            collective_id=0, has_side_effects=True, vmem_limit_bytes=60 * 1024 * 1024
        ),
    )(docs, layers, handed, gate, key, inputs, filters, *fixed)


def body(handed_back, gate_q, key_k, input_x, filter_h, doc_lengths, section_layers):
    channels, width = gate_q.shape[2:]
    blocks = lax.axis_size("ctx")
    shape = (blocks, channels // blocks, width)
    blocked = [v.reshape(shape) for v in (handed_back, gate_q, key_k, input_x, filter_h)]
    incoming, conv, both, live, scale = mixer(doc_lengths, section_layers, *blocked)
    corr, lags = [both[:, :, i].reshape(shape) for i in range(2)]
    live, scale = live[None], scale[None]
    key32 = blocked[2].astype(jnp.float32)
    input32 = blocked[3].astype(jnp.float32)
    grad32 = incoming.astype(jnp.float32)
    corr32 = corr.astype(jnp.float32)
    grad_gate = (scale * grad32 * conv.astype(jnp.float32)).astype(jnp.bfloat16)
    grad_key = (corr32 * input32 * live).astype(jnp.bfloat16)
    grad_input = (grad32 + corr32 * key32 * live).astype(jnp.bfloat16)
    grad_filter = lags.astype(jnp.float32) / math.sqrt(blocks * width)
    flat = gate_q.shape
    return (
        grad_input.reshape(flat),
        grad_gate.reshape(flat),
        grad_key.reshape(flat),
        grad_filter.reshape(filter_h.shape),
    )


def solution(mesh):
    return jax.shard_map(
        body,
        mesh=mesh,
        in_specs=(
            P("pipe", None, "chan", "ctx"),
            P("pipe", None, "chan", "ctx"),
            P("pipe", None, "chan", "ctx"),
            P("pipe", None, "chan", "ctx"),
            P("pipe", "chan", "ctx"),
            P(),
            P(),
        ),
        out_specs=(
            P("pipe", None, "chan", "ctx"),
            P("pipe", None, "chan", "ctx"),
            P("pipe", None, "chan", "ctx"),
            P("pipe", "chan", "ctx"),
        ),
        check_vma=False,
    )
```

```python
import functools
import math

import jax
import jax.numpy as jnp
import numpy as np
from jax import lax
from jax.experimental import pallas as pl
from jax.experimental.pallas import tpu as pltpu
from jax.sharding import PartitionSpec as P

GROUP = 8


def halves(table):
    top = table.astype(jnp.bfloat16)
    rest = (table - top.astype(np.float64)).astype(jnp.bfloat16)
    return np.stack([top, rest])


@functools.lru_cache(maxsize=None)
def tables(blocks, width):
    length = blocks * width
    turn = 2.0 * math.pi
    row = np.arange(blocks)[:, None]
    quarter = np.arange(blocks)[:, None] + 0.25
    outer = turn * quarter * row.T / blocks
    wave = np.concatenate([np.cos(outer), -np.sin(outer)])
    spread = np.kron(wave, np.eye(GROUP))
    twist = np.repeat(turn * quarter * np.arange(width)[None, :] / length, GROUP, axis=0)
    lane = np.arange(width)
    inner = turn * ((lane[:, None] * lane[None, :]) % width) / width
    cos, sin = np.cos(inner), np.sin(inner)
    ahead = np.block([[cos, -sin], [sin, cos]])
    back = np.block([[cos, sin], [-sin, cos]])
    turns = np.stack([np.cos(twist), -np.sin(twist)]).astype(np.float32)
    return (halves(spread), halves(spread.T / length), halves(ahead), halves(back), turns)


def fixed_left(table_ref, right):
    return jnp.dot(table_ref[0], right, preferred_element_type=jnp.float32) + jnp.dot(
        table_ref[1], right, preferred_element_type=jnp.float32
    )


def fixed_right(left, table_ref):
    return jnp.dot(left, table_ref[0], preferred_element_type=jnp.float32) + jnp.dot(
        left, table_ref[1], preferred_element_type=jnp.float32
    )


def transform(wide_ref, spec_ref, span, spread_ref, ahead_ref, turns_ref):
    blocks, channels, width = wide_ref.shape
    rows = blocks * GROUP
    first, count = span
    for start in range(first, first + count, 2):
        groups = range(start, min(start + 2, first + count))
        chunk = wide_ref[:, GROUP * start : GROUP * (groups[-1] + 1), :].astype(jnp.float32)
        sides = [
            chunk[:, GROUP * (g - start) : GROUP * (g - start + 1), :].reshape(rows, width)
            for g in groups
        ]
        mixed = fixed_left(spread_ref, jnp.concatenate(sides, axis=1).astype(jnp.bfloat16))
        for side, group in enumerate(groups):
            part = mixed[:, side * width : (side + 1) * width]
            part_re, part_im = part[:rows], part[rows:]
            turned = jnp.concatenate(
                [
                    part_re * turns_ref[0] - part_im * turns_ref[1],
                    part_re * turns_ref[1] + part_im * turns_ref[0],
                ],
                axis=1,
            )
            spec_ref[group] = fixed_right(turned.astype(jnp.bfloat16), ahead_ref)


def multiply(left_ref, right_ref, conjugate, wide_ref, span, gather_ref, back_ref, turns_ref):
    blocks, channels, width = wide_ref.shape
    first, count = span
    for start in range(first, first + count, 2):
        groups = range(start, min(start + 2, first + count))
        sides = []
        for group in groups:
            left, right = left_ref[group], right_ref[group]
            left_re, left_im = left[:, :width], left[:, width:]
            right_re, right_im = right[:, :width], right[:, width:]
            if conjugate:
                left_im = -left_im
            both = jnp.concatenate(
                [left_re * right_re - left_im * right_im, left_re * right_im + left_im * right_re],
                axis=1,
            )
            part = fixed_right(both.astype(jnp.bfloat16), back_ref)
            part_re, part_im = part[:, :width], part[:, width:]
            sides.append(
                jnp.concatenate(
                    [
                        part_re * turns_ref[0] + part_im * turns_ref[1],
                        part_im * turns_ref[0] - part_re * turns_ref[1],
                    ],
                    axis=0,
                )
            )
        signal = fixed_left(gather_ref, jnp.concatenate(sides, axis=1).astype(jnp.bfloat16))
        outs = [
            signal[:, s * width : (s + 1) * width].reshape(blocks, GROUP, width)
            for s in range(len(sides))
        ]
        chunk = jnp.concatenate(outs, axis=1).astype(jnp.bfloat16)
        wide_ref[:, GROUP * (start - first) : GROUP * (groups[-1] + 1 - first), :] = chunk


MESH = pl.DeviceIdType.MESH
PIECES = 2
STRIDE = 13
OUTWARD, CONV, GRAD, BACK = 0, 1, 2, 2 + PIECES
STREAMS = 2 + 2 * PIECES
LOADS = 9


def kernel(
    docs_ref, layers_ref, handed_ref, gate_home, key_home, input_home, filter_ref,
    spread_home, gather_home, ahead_home, back_home, turns_home,
    incoming_ref, conv_ref, corr_ref, lag_ref, live_ref, scale_ref,
    first_out, first_wide, grad_out, grad_wide, conv_wide, both_wide, both_ref,
    filter_spec, prod_spec, grad_spec,
    gate_ref, key_ref, input_ref, spread_ref, gather_ref, ahead_ref, back_ref, turns_ref,
    send_sems, recv_sems, relay_send, relay_recv, load_sems,
):
    blocks, channels, width = key_ref.shape
    me = lax.axis_index("ctx")
    section, sections = lax.axis_index("pipe"), lax.axis_size("pipe")
    before = lax.rem(section + sections - 1, sections)
    after = lax.rem(section + 1, sections)
    share = channels // PIECES
    every = (0, channels // GROUP)

    def part(ref, piece):
        return ref.at[:, pl.ds(share * piece, share), :]

    def groups(piece):
        return (share * piece // GROUP, share // GROUP)

    def relay(piece):
        return pltpu.make_async_remote_copy(
            src_ref=part(handed_ref, piece),
            dst_ref=part(incoming_ref, piece),
            send_sem=relay_send.at[piece],
            recv_sem=relay_recv.at[piece],
            device_id={"pipe": before},
            device_id_type=MESH,
        )

    def scatter(source, target, stream):
        def step(index, carry):
            peer = lax.rem(me + STRIDE * index, blocks)
            pltpu.make_async_remote_copy(
                src_ref=source.at[peer],
                dst_ref=target.at[me],
                send_sem=send_sems.at[stream],
                recv_sem=recv_sems.at[stream],
                device_id={"ctx": peer},
                device_id_type=MESH,
            ).start()
            return carry

        lax.fori_loop(1, blocks, step, 0)
        target[me] = source[me]

    def settle(buffer, stream):
        others = buffer.at[pl.ds(0, blocks - 1)]
        return pltpu.make_async_remote_copy(
            src_ref=others,
            dst_ref=others,
            send_sem=send_sems.at[stream],
            recv_sem=recv_sems.at[stream],
            device_id={"ctx": lax.rem(me + 1, blocks)},
            device_id_type=MESH,
        )

    loads = [
        pltpu.make_async_copy(source, target, load_sems.at[index])
        for index, (source, target) in enumerate(
            [
                (key_home, key_ref),
                (input_home, input_ref),
                (filter_ref, first_out.at[:, 0]),
                (spread_home, spread_ref),
                (ahead_home, ahead_ref),
                (turns_home, turns_ref),
                (back_home, back_ref),
                (gather_home, gather_ref),
                (gate_home, gate_ref),
            ]
        )
    ]
    barrier = pltpu.get_barrier_semaphore()

    def greet(index, carry):
        pl.semaphore_signal(
            barrier, inc=1, device_id={"ctx": lax.rem(me + index, blocks)}, device_id_type=MESH
        )
        return carry

    for neighbour in (before, after):
        pl.semaphore_signal(barrier, inc=1, device_id={"pipe": neighbour}, device_id_type=MESH)
    lax.fori_loop(1, blocks, greet, 0)
    for load in loads:
        load.start()

    spots = me * width + lax.broadcasted_iota(jnp.int32, live_ref.shape, 1)
    limit = blocks * width - docs_ref[0, docs_ref.shape[1] - 1]
    live_ref[...] = (spots < limit).astype(jnp.float32)
    layers = jnp.full(scale_ref.shape, layers_ref[section], jnp.int32)
    scale_ref[...] = 1.0 / jnp.sqrt(layers.astype(jnp.float32))
    live = live_ref[...][None]
    scale = scale_ref[...][None]
    for load in loads[:3]:
        load.wait()
    first_out[:, 1] = (
        key_ref[...].astype(jnp.float32) * input_ref[...].astype(jnp.float32) * live
    ).astype(jnp.bfloat16)
    pl.semaphore_wait(barrier, blocks + 1)

    for piece in range(PIECES):
        relay(piece).start()
    scatter(first_out, first_wide, OUTWARD)
    for load in loads[3:]:
        load.wait()
    settle(first_wide, OUTWARD).wait_recv()
    transform(first_wide.at[:, 0], filter_spec, every, spread_ref, ahead_ref, turns_ref)
    transform(first_wide.at[:, 1], prod_spec, every, spread_ref, ahead_ref, turns_ref)
    multiply(filter_spec, prod_spec, False, conv_wide, every, gather_ref, back_ref, turns_ref)
    scatter(conv_wide, conv_ref, CONV)

    def send_grad(piece):
        relay(piece).wait_recv()
        span = pl.ds(share * piece, share)
        grad_out[:, span, :] = (
            scale
            * gate_ref[:, span, :].astype(jnp.float32)
            * incoming_ref[:, span, :].astype(jnp.float32)
        ).astype(jnp.bfloat16)
        scatter(part(grad_out, piece), part(grad_wide, piece), GRAD + piece)

    def send_back(piece):
        span = groups(piece)
        settle(part(grad_wide, piece), GRAD + piece).wait_recv()
        transform(grad_wide, grad_spec, span, spread_ref, ahead_ref, turns_ref)
        for index, spec in enumerate((filter_spec, prod_spec)):
            multiply(
                spec, grad_spec, True, both_wide.at[:, piece, index], span,
                gather_ref, back_ref, turns_ref,
            )
        scatter(both_wide.at[:, piece], both_ref.at[:, piece], BACK + piece)

    for piece in range(PIECES):
        send_grad(piece)
    for piece in range(PIECES):
        send_back(piece)

    settle(conv_ref, CONV).wait()
    settle(first_wide, OUTWARD).wait_send()
    for piece in range(PIECES):
        relay(piece).wait_send()
        settle(part(grad_wide, piece), GRAD + piece).wait_send()
        settle(both_ref.at[:, piece], BACK + piece).wait()
        span = pl.ds(share * piece, share)
        corr_ref[:, span, :] = both_ref[:, piece, 0]
        lag_ref[:, span, :] = both_ref[:, piece, 1]


def mixer(docs, layers, handed, gate, key, inputs, filters):
    blocks, channels, width = key.shape
    moved = jax.ShapeDtypeStruct(key.shape, jnp.bfloat16)
    both = (blocks, PIECES, 2, channels // PIECES, width)
    line = jax.ShapeDtypeStruct((1, width), jnp.float32)
    wide = pltpu.VMEM(key.shape, jnp.bfloat16)
    double = pltpu.VMEM((blocks, 2, channels, width), jnp.bfloat16)
    spec = pltpu.VMEM((channels // GROUP, blocks * GROUP, 2 * width), jnp.float32)
    held = pl.BlockSpec(memory_space=pltpu.VMEM)
    small = pl.BlockSpec(memory_space=pltpu.SMEM)
    far = pl.BlockSpec(memory_space=pl.ANY)
    fixed = tables(blocks, width)
    return pl.pallas_call(
        kernel,
        out_shape=(moved, moved, moved, moved, line, line),
        in_specs=[small] * 2 + [far] * 10,
        out_specs=(held,) * 6,
        scratch_shapes=[double, double, wide, wide, wide]
        + [pltpu.VMEM(both, jnp.bfloat16)] * 2
        + [spec] * 3
        + [wide] * 3
        + [pltpu.VMEM(table.shape, table.dtype) for table in fixed]
        + [
            pltpu.SemaphoreType.DMA((STREAMS,)),
            pltpu.SemaphoreType.DMA((STREAMS,)),
            pltpu.SemaphoreType.DMA((PIECES,)),
            pltpu.SemaphoreType.DMA((PIECES,)),
            pltpu.SemaphoreType.DMA((LOADS,)),
        ],
        compiler_params=pltpu.CompilerParams(
            collective_id=0, has_side_effects=True, vmem_limit_bytes=60 * 1024 * 1024
        ),
    )(docs, layers, handed, gate, key, inputs, filters, *fixed)


def body(handed_back, gate_q, key_k, input_x, filter_h, doc_lengths, section_layers):
    channels, width = gate_q.shape[2:]
    blocks = lax.axis_size("ctx")
    shape = (blocks, channels // blocks, width)
    blocked = [v.reshape(shape) for v in (handed_back, gate_q, key_k, input_x, filter_h)]
    incoming, conv, corr, lags, live, scale = mixer(doc_lengths, section_layers, *blocked)
    live, scale = live[None], scale[None]
    key32 = blocked[2].astype(jnp.float32)
    input32 = blocked[3].astype(jnp.float32)
    grad32 = incoming.astype(jnp.float32)
    corr32 = corr.astype(jnp.float32)
    grad_gate = (scale * grad32 * conv.astype(jnp.float32)).astype(jnp.bfloat16)
    grad_key = (corr32 * input32 * live).astype(jnp.bfloat16)
    grad_input = (grad32 + corr32 * key32 * live).astype(jnp.bfloat16)
    grad_filter = lags.astype(jnp.float32) / math.sqrt(blocks * width)
    flat = gate_q.shape
    return (
        grad_input.reshape(flat),
        grad_gate.reshape(flat),
        grad_key.reshape(flat),
        grad_filter.reshape(filter_h.shape),
    )


def solution(mesh):
    return jax.shard_map(
        body,
        mesh=mesh,
        in_specs=(
            P("pipe", None, "chan", "ctx"),
            P("pipe", None, "chan", "ctx"),
            P("pipe", None, "chan", "ctx"),
            P("pipe", None, "chan", "ctx"),
            P("pipe", "chan", "ctx"),
            P(),
            P(),
        ),
        out_specs=(
            P("pipe", None, "chan", "ctx"),
            P("pipe", None, "chan", "ctx"),
            P("pipe", None, "chan", "ctx"),
            P("pipe", "chan", "ctx"),
        ),
        check_vma=False,
    )
```
